32 devices in a mesh: depth: 4 (over z), row: 4 (over x, core), col: 2 (over y).
Axes of the slice: x: 2, y: 2, z: 4, core: 2. Of those that a mesh axis runs over, the one named last changes fastest.
Arguments:
- acts: bfloat16 [2048, 4096], P(('depth', 'col'), 'row'), may hold values from -0.3125 to 0.3125
- grad_out: bfloat16 [2048, 14336], P(('depth', 'row'), 'col'), may hold values from -6 to 6
- weight: bfloat16 [4096, 14336], P('row', 'col'), may hold values from -0.046875 to 0.046875
Outputs:
- grad_acts: bfloat16 [2048, 4096], P(('depth', 'col'), 'row')
- grad_weight: bfloat16 [4096, 14336], P('row', 'col')
The draws below stay inside these ranges and needn't reach their ends.
All inputs are finite; a program needn't handle non-finite values.
Results may differ from the reference program's by a relative error of at most 0.013.
Values may be sent and summed in bfloat16 or wider, within the bound.
A program may use at most 128 MiB of HBM per device.

```python
import jax
import jax.numpy as jnp

D = 4096
F = 14336
TOKENS = 2048
N_DEPTH = 4
N_COL = 2


def level_of(own_key, dims, cuts, low, high):
    loudness, own = 1.0, jax.random.fold_in(own_key, 6)
    for axis_at, shards_of in cuts:
        heights = jnp.exp(jax.random.uniform(jax.random.fold_in(own, axis_at), (shards_of,), jnp.float32, low / len(cuts), high / len(cuts)))
        loudness = loudness * jnp.repeat(heights, dims[axis_at] // shards_of).reshape([-1 if axis == axis_at else 1 for axis in range(len(dims))])
    return loudness


def gaussian(stream_key, dims, width, most, pieces=(), held_as=jnp.bfloat16):
    gain = level_of(stream_key, dims, pieces, -0.22, 0.18) if pieces else 1.0
    array = jax.random.normal(stream_key, dims, jnp.float32) * width * gain
    return jnp.minimum(jnp.maximum(array, -most), most).astype(held_as)


def setup_inputs(seed: int = 0) -> dict:
    splits = jax.random.split(jax.random.key(seed), 4)
    return {
        "acts": gaussian(splits[0], (TOKENS, D), (TOKENS ** -0.5), 0.3125, ((0, 8), (1, 4))),
        "grad_out": gaussian(splits[1], (TOKENS, F), 1.0, 6.0, ((0, 16), (1, 2))),
        "weight": gaussian(splits[2], (D, F), F ** -0.5, 0.046875, ((0, 4), (1, 2))),
    }


def reference(acts, grad_out, weight):
    block = F // N_COL
    grad_acts = jnp.zeros((TOKENS, D), jnp.float32)
    for index in range(N_COL):
        piece = grad_out[:, index * block:(index + 1) * block]
        wpart = weight[:, index * block:(index + 1) * block]
        term = jnp.dot(piece, wpart.T, preferred_element_type=jnp.float32).astype(jnp.bfloat16)
        grad_acts = grad_acts + term.astype(jnp.float32)
    layer = TOKENS // N_DEPTH
    grad_weight = jnp.zeros((D, F), jnp.float32)
    for index in range(N_DEPTH):
        rows_a = acts[index * layer:(index + 1) * layer]
        rows_g = grad_out[index * layer:(index + 1) * layer]
        term = jnp.dot(rows_a.T, rows_g, preferred_element_type=jnp.float32).astype(jnp.bfloat16)
        grad_weight = grad_weight + term.astype(jnp.float32)
    return grad_acts.astype(jnp.bfloat16), grad_weight.astype(jnp.bfloat16)
```

```python
import functools

import jax
import jax.numpy as jnp
from jax import lax
from jax.experimental import pallas as pl
from jax.experimental.pallas import tpu as pltpu
from jax.sharding import PartitionSpec as P

MESH = pl.DeviceIdType.MESH
CORES = 2


def kernel(nd, nr, nc, nch, cols, at_ref, g_ref, w_ref, ga_ref, gw_ref,
           grads, acts, total, term, parts, wbuf, obuf,
           recv_g, recv_a, recv_t, send_g, send_a, send_t, load_sem, w_sem, o_sem):
    nx = nr // CORES
    l, r, c = lax.axis_index("depth"), lax.axis_index("row"), lax.axis_index("col")
    core = lax.rem(r, CORES)
    xi = lax.div(r, CORES)
    partner = xi * CORES + (1 - core)
    xpeers = [lax.rem(xi + o, nx) * CORES + core for o in range(1, nx)]
    cpeers = [lax.rem(c + o, nc) for o in range(1, nc)]
    rows = g_ref.shape[0]
    width = at_ref.shape[1]
    feats = at_ref.shape[0]
    layer = nr * rows
    block = layer // nc
    UP, DOWN, CORE, X = 0, 1, 2, 3

    def piece(p, j):
        return grads.at[j, pl.ds(pl.multiple_of(p * rows, rows), rows), :]

    def whole(p):
        return grads.at[:, pl.ds(pl.multiple_of(p * rows, rows), rows), :]

    def apiece(q):
        return acts.at[:, pl.ds(pl.multiple_of(q * width, width), width)]

    def g_copy(p, j, way, dev):
        return pltpu.make_async_remote_copy(
            src_ref=piece(p, j), dst_ref=piece(p, j), send_sem=send_g.at[way, p],
            recv_sem=recv_g.at[p, j], device_id=dev, device_id_type=MESH)

    def a_copy(q, way, dev):
        return pltpu.make_async_remote_copy(
            src_ref=apiece(q), dst_ref=apiece(q), send_sem=send_a.at[way, q],
            recv_sem=recv_a.at[q], device_id=dev, device_id_type=MESH)

    def g_wait(p, j):
        pltpu.make_async_copy(piece(p, j), piece(p, j), recv_g.at[p, j]).wait()

    def a_wait(q):
        pltpu.make_async_copy(apiece(q), apiece(q), recv_a.at[q]).wait()

    def to_x(p, j):
        for o, dev in enumerate(xpeers):
            g_copy(p, j, X + o, {"row": dev}).start()

    def to_core(p, j):
        g_copy(p, j, CORE, {"row": partner}).start()

    def to_up(p, j):
        @pl.when(l < nd - 1)
        def _():
            g_copy(p, j, UP, {"depth": l + 1}).start()

    def to_down(p, j):
        @pl.when(l > 0)
        def _():
            g_copy(p, j, DOWN, {"depth": l - 1}).start()

    def w_copy(j):
        return pltpu.make_async_copy(
            w_ref.at[:, pl.ds(pl.multiple_of(j * cols, cols), cols)], wbuf.at[lax.rem(j, 2)],
            w_sem.at[lax.rem(j, 2)])

    def o_copy(j):
        return pltpu.make_async_copy(
            obuf.at[lax.rem(j, 2)], gw_ref.at[:, pl.ds(pl.multiple_of(j * cols, cols), cols)],
            o_sem.at[lax.rem(j, 2)])

    own = l * nr + r
    mine = l * nc + c

    @pl.loop(0, nch)
    def _(j):
        pltpu.make_async_copy(
            g_ref.at[:, pl.ds(pl.multiple_of(j * cols, cols), cols)], piece(own, j), load_sem.at[0]).start()

    own_acts = pltpu.make_async_copy(at_ref, apiece(mine), load_sem.at[1])
    own_acts.start()
    w_copy(0).start()

    barrier = pltpu.get_barrier_semaphore()
    peers = [{"row": partner}] + [{"row": x} for x in xpeers] + [{"col": y} for y in cpeers]
    for dev in peers:
        pl.semaphore_signal(barrier, inc=1, device_id=dev, device_id_type=MESH)

    @pl.when(l > 0)
    def _():
        pl.semaphore_signal(barrier, inc=1, device_id={"depth": l - 1}, device_id_type=MESH)

    @pl.when(l < nd - 1)
    def _():
        pl.semaphore_signal(barrier, inc=1, device_id={"depth": l + 1}, device_id_type=MESH)

    neighbours = jnp.where(l > 0, 1, 0) + jnp.where(l < nd - 1, 1, 0)
    pl.semaphore_wait(barrier, len(peers) + neighbours)

    own_acts.wait()
    pltpu.make_async_copy(whole(own), whole(own), load_sem.at[0]).wait()

    @pl.when(l < nd - 1)
    def _():
        a_copy(mine, UP, {"depth": l + 1}).start()

    @pl.when(l > 0)
    def _():
        a_copy(mine, DOWN, {"depth": l - 1}).start()

    for o, dev in enumerate(cpeers):
        a_copy(mine, 2 + o, {"col": dev}).start()

    to_up(own, 0)
    to_down(own, 0)

    @pl.loop(0, nch)
    def _(j):
        to_x(own, j)
        to_core(own, j)

    total[...] = jnp.zeros_like(total)

    tile_f = 256

    def step(s, carry):
        @pl.when(s + 1 < nch)
        def _():
            to_up(own, s + 1)
            to_down(own, s + 1)

        for d in range(1, nd):
            j = s - d
            live = (j >= 0) & (j < nch)
            for sign, onward in ((-1, to_up), (1, to_down)):
                src = l + sign * d
                there = (src >= 0) if sign < 0 else (src < nd)

                @pl.when(live & there)
                def _(j=j, src=src, onward=onward):
                    p = src * nr + r
                    g_wait(p, j)
                    onward(p, j)
                    to_x(p, j)
                    to_core(p, j)

                @pl.when((s == d) & there)
                def _(src=src, sign=sign):
                    q = src * nc + c
                    a_wait(q)
                    if sign < 0:
                        @pl.when(l < nd - 1)
                        def _():
                            a_copy(q, UP, {"depth": l + 1}).start()
                    else:
                        @pl.when(l > 0)
                        def _():
                            a_copy(q, DOWN, {"depth": l - 1}).start()
                    for o, dev in enumerate(cpeers):
                        a_copy(q, 2 + o, {"col": dev}).start()

        for d in range(0, nd):
            j = s - (d + 1 if d else 0)
            live = (j >= 0) & (j < nch)
            for sign in ((-1, 1) if d else (1,)):
                src = l + sign * d
                there = (src >= 0) & (src < nd)

                @pl.when(live & there)
                def _(j=j, src=src):
                    for x in xpeers:
                        g_wait(src * nr + x, j)
                        to_core(src * nr + x, j)

        j1 = s - 1

        @pl.when((j1 >= 0) & (j1 < nch))
        def _():
            for x in range(nx):
                g_wait(l * nr + x * CORES + 1 - core, j1)
            w_copy(j1).wait()

            @pl.when(j1 + 1 < nch)
            def _():
                w_copy(j1 + 1).start()

            lhs = grads[j1, pl.ds(pl.multiple_of(l * layer, layer), layer), :]

            @pl.loop(0, feats // tile_f)
            def _(i):
                at = pl.ds(pl.multiple_of(i * tile_f, tile_f), tile_f)
                total[:, at] += lax.dot_general(
                    lhs, wbuf[lax.rem(j1, 2), at, :], (((1,), (1,)), ((), ())),
                    preferred_element_type=jnp.float32)

        @pl.when(s == nch)
        def _():
            term[...] = total[...].astype(term.dtype)

        @pl.when(s == nch + 1)
        def _():
            for o, dev in enumerate(cpeers):
                pltpu.make_async_remote_copy(
                    src_ref=term.at[pl.ds(pl.multiple_of(dev * block, block), block), :],
                    dst_ref=parts.at[o], send_sem=send_t.at[o], recv_sem=recv_t.at[o],
                    device_id={"col": dev}, device_id_type=MESH).start()

        j2 = s - (nd + 1)

        @pl.when(j2 == 0)
        def _():
            for k in range(nd):
                for dev in cpeers:
                    a_wait(k * nc + dev)

        @pl.when(j2 >= 0)
        def _():
            for k in range(1, nd):
                for x in range(nx):
                    g_wait(lax.rem(l + k, nd) * nr + x * CORES + 1 - core, j2)

            @pl.when(j2 >= 2)
            def _():
                o_copy(j2 - 2).wait()

            @pl.loop(0, feats // tile_f)
            def _(i):
                at = pl.ds(pl.multiple_of(i * tile_f, tile_f), tile_f)
                obuf[lax.rem(j2, 2), at, :] = jnp.dot(
                    acts[at, :], grads[j2], preferred_element_type=jnp.float32).astype(obuf.dtype)

            o_copy(j2).start()

        return carry

    lax.fori_loop(0, nch + nd + 1, step, 0)

    result = total[pl.ds(pl.multiple_of(c * block, block), block), :]
    for o, dev in enumerate(cpeers):
        pltpu.make_async_copy(parts.at[o], parts.at[o], recv_t.at[o]).wait()
        result = result + parts[o].astype(jnp.float32)
    ga_ref[...] = result.astype(ga_ref.dtype)

    for o, dev in enumerate(cpeers):
        pltpu.make_async_copy(parts.at[o], parts.at[o], send_t.at[o]).wait()

    def sent_g(way, p):
        pltpu.make_async_copy(whole(p), whole(p), send_g.at[way, p]).wait()

    def sent_a(way, q):
        pltpu.make_async_copy(apiece(q), apiece(q), send_a.at[way, q]).wait()

    for k in range(nd):
        p, q = k * nr + r, k * nc + c

        @pl.when((k <= l) & (l < nd - 1))
        def _(p=p, q=q):
            sent_g(UP, p)
            sent_a(UP, q)

        @pl.when((k >= l) & (l > 0))
        def _(p=p, q=q):
            sent_g(DOWN, p)
            sent_a(DOWN, q)

        for o in range(len(xpeers)):
            sent_g(X + o, p)
        for x in range(nx):
            sent_g(CORE, k * nr + x * CORES + core)
        for o in range(len(cpeers)):
            sent_a(2 + o, q)

    if nch >= 2:
        o_copy(nch - 2).wait()
    o_copy(nch - 1).wait()


def shards(nd, nr, nc, acts, grad_out, weight):
    rows, width = grad_out.shape
    cols = 512 if width % 512 == 0 else 256
    nch = width // cols
    feats = acts.shape[1]
    layer = nr * rows
    block = layer // nc
    bf16, dma = jnp.bfloat16, pltpu.SemaphoreType.DMA
    anywhere = pl.BlockSpec(memory_space=pl.ANY)
    nx = nr // CORES
    pieces, apieces = nd * nr, nd * nc
    return pl.pallas_call(
        functools.partial(kernel, nd, nr, nc, nch, cols),
        out_shape=(
            jax.ShapeDtypeStruct((block, feats), bf16),
            jax.ShapeDtypeStruct((feats, width), bf16),
        ),
        in_specs=[anywhere] * 3,
        out_specs=(pl.BlockSpec(memory_space=pltpu.VMEM), anywhere),
        scratch_shapes=[
            pltpu.VMEM((nch, pieces * rows, cols), bf16),
            pltpu.VMEM((feats, apieces * acts.shape[0]), bf16),
            pltpu.VMEM((layer, feats), jnp.float32),
            pltpu.VMEM((layer, feats), bf16),
            pltpu.VMEM((nc - 1, block, feats), bf16),
            pltpu.VMEM((2, feats, cols), bf16),
            pltpu.VMEM((2, feats, cols), bf16),
            dma((pieces, nch)), dma((apieces,)), dma((nc - 1,)),
            dma((3 + nx - 1, pieces)), dma((2 + nc - 1, apieces)), dma((nc - 1,)),
            dma((2,)), dma((2,)), dma((2,)),
        ],
        compiler_params=pltpu.CompilerParams(
            collective_id=0, has_side_effects=True, vmem_limit_bytes=67_043_328),
    )(acts.T, grad_out, weight)


def solution(mesh):
    nd, nr, nc = mesh.shape["depth"], mesh.shape["row"], mesh.shape["col"]
    in_specs = (P(("depth", "col"), "row"), P(("depth", "row"), "col"), P("row", "col"))
    out_specs = (P(("depth", "col"), "row"), P("row", "col"))
    return jax.shard_map(functools.partial(shards, nd, nr, nc), mesh=mesh,
                         in_specs=in_specs, out_specs=out_specs, check_vma=False)
```

```python
import functools

import jax
import jax.numpy as jnp
from jax import lax
from jax.experimental import pallas as pl
from jax.experimental.pallas import tpu as pltpu
from jax.sharding import PartitionSpec as P

MESH = pl.DeviceIdType.MESH
CORES = 2


def kernel(nd, nr, nc, nch, late, cols, at_ref, g_ref, w_ref, ga_ref, gw_ref, all_ref, last_ref,
           grads, acts, total, term, parts, wbuf, obuf,
           recv_g, recv_a, recv_t, send_g, send_a, send_t, load_sem, w_sem, o_sem, all_sem, last_sem):
    nx = nr // CORES
    l, r, c = lax.axis_index("depth"), lax.axis_index("row"), lax.axis_index("col")
    core = lax.rem(r, CORES)
    xi = lax.div(r, CORES)
    partner = xi * CORES + (1 - core)
    xpeers = [lax.rem(xi + o, nx) * CORES + core for o in range(1, nx)]
    cpeers = [lax.rem(c + o, nc) for o in range(1, nc)]
    rows = g_ref.shape[0]
    width = at_ref.shape[1]
    feats = at_ref.shape[0]
    layer = nr * rows
    block = layer // nc
    UP, DOWN, CORE, X = 0, 1, 2, 3

    def piece(p, j):
        return grads.at[j, pl.ds(pl.multiple_of(p * rows, rows), rows), :]

    def whole(p):
        return grads.at[:, pl.ds(pl.multiple_of(p * rows, rows), rows), :]

    def apiece(q):
        return acts.at[:, pl.ds(pl.multiple_of(q * width, width), width)]

    def g_copy(p, j, way, dev):
        return pltpu.make_async_remote_copy(
            src_ref=piece(p, j), dst_ref=piece(p, j), send_sem=send_g.at[way, p],
            recv_sem=recv_g.at[p, j], device_id=dev, device_id_type=MESH)

    def a_copy(q, way, dev):
        return pltpu.make_async_remote_copy(
            src_ref=apiece(q), dst_ref=apiece(q), send_sem=send_a.at[way, q],
            recv_sem=recv_a.at[q], device_id=dev, device_id_type=MESH)

    def g_wait(p, j):
        pltpu.make_async_copy(piece(p, j), piece(p, j), recv_g.at[p, j]).wait()

    def a_wait(q):
        pltpu.make_async_copy(apiece(q), apiece(q), recv_a.at[q]).wait()

    def to_x(p, j):
        for o, dev in enumerate(xpeers):
            g_copy(p, j, X + o, {"row": dev}).start()

    def to_core(p, j):
        g_copy(p, j, CORE, {"row": partner}).start()

    def to_up(p, j):
        @pl.when(l < nd - 1)
        def _():
            g_copy(p, j, UP, {"depth": l + 1}).start()

    def to_down(p, j):
        @pl.when(l > 0)
        def _():
            g_copy(p, j, DOWN, {"depth": l - 1}).start()

    def w_copy(j):
        return pltpu.make_async_copy(
            w_ref.at[:, pl.ds(pl.multiple_of(j * cols, cols), cols)], wbuf.at[lax.rem(j, 2)],
            w_sem.at[lax.rem(j, 2)])

    def o_copy(j):
        return pltpu.make_async_copy(
            obuf.at[lax.rem(j, 2)], gw_ref.at[:, pl.ds(pl.multiple_of(j * cols, cols), cols)],
            o_sem.at[lax.rem(j, 2)])

    def last_copy(i):
        return pltpu.make_async_copy(
            grads.at[nch - late + i], last_ref.at[:, pl.ds(pl.multiple_of(i * cols, cols), cols)],
            last_sem.at[i])

    all_copy = pltpu.make_async_copy(acts, all_ref, all_sem)

    own = l * nr + r
    mine = l * nc + c

    @pl.loop(0, nch)
    def _(j):
        pltpu.make_async_copy(
            g_ref.at[:, pl.ds(pl.multiple_of(j * cols, cols), cols)], piece(own, j), load_sem.at[0]).start()

    own_acts = pltpu.make_async_copy(at_ref, apiece(mine), load_sem.at[1])
    own_acts.start()
    w_copy(0).start()

    barrier = pltpu.get_barrier_semaphore()
    peers = [{"row": partner}] + [{"row": x} for x in xpeers] + [{"col": y} for y in cpeers]
    for dev in peers:
        pl.semaphore_signal(barrier, inc=1, device_id=dev, device_id_type=MESH)

    @pl.when(l > 0)
    def _():
        pl.semaphore_signal(barrier, inc=1, device_id={"depth": l - 1}, device_id_type=MESH)

    @pl.when(l < nd - 1)
    def _():
        pl.semaphore_signal(barrier, inc=1, device_id={"depth": l + 1}, device_id_type=MESH)

    neighbours = jnp.where(l > 0, 1, 0) + jnp.where(l < nd - 1, 1, 0)
    pl.semaphore_wait(barrier, len(peers) + neighbours)

    own_acts.wait()
    pltpu.make_async_copy(whole(own), whole(own), load_sem.at[0]).wait()

    @pl.when(l < nd - 1)
    def _():
        a_copy(mine, UP, {"depth": l + 1}).start()

    @pl.when(l > 0)
    def _():
        a_copy(mine, DOWN, {"depth": l - 1}).start()

    for o, dev in enumerate(cpeers):
        a_copy(mine, 2 + o, {"col": dev}).start()

    to_up(own, 0)
    to_down(own, 0)

    @pl.loop(0, nch)
    def _(j):
        to_x(own, j)
        to_core(own, j)

    total[...] = jnp.zeros_like(total)

    tile_f = 256

    def step(s, carry):
        @pl.when(s + 1 < nch)
        def _():
            to_up(own, s + 1)
            to_down(own, s + 1)

        for d in range(1, nd):
            j = s - d
            live = (j >= 0) & (j < nch)
            for sign, onward in ((-1, to_up), (1, to_down)):
                src = l + sign * d
                there = (src >= 0) if sign < 0 else (src < nd)

                @pl.when(live & there)
                def _(j=j, src=src, onward=onward):
                    p = src * nr + r
                    g_wait(p, j)
                    onward(p, j)
                    to_x(p, j)
                    to_core(p, j)

                @pl.when((s == d) & there)
                def _(src=src, sign=sign):
                    q = src * nc + c
                    a_wait(q)
                    if sign < 0:
                        @pl.when(l < nd - 1)
                        def _():
                            a_copy(q, UP, {"depth": l + 1}).start()
                    else:
                        @pl.when(l > 0)
                        def _():
                            a_copy(q, DOWN, {"depth": l - 1}).start()
                    for o, dev in enumerate(cpeers):
                        a_copy(q, 2 + o, {"col": dev}).start()

        for d in range(0, nd):
            j = s - (d + 1 if d else 0)
            live = (j >= 0) & (j < nch)
            for sign in ((-1, 1) if d else (1,)):
                src = l + sign * d
                there = (src >= 0) & (src < nd)

                @pl.when(live & there)
                def _(j=j, src=src):
                    for x in xpeers:
                        g_wait(src * nr + x, j)
                        to_core(src * nr + x, j)

        j1 = s - 1

        @pl.when((j1 >= 0) & (j1 < nch))
        def _():
            for x in range(nx):
                g_wait(l * nr + x * CORES + 1 - core, j1)
            w_copy(j1).wait()

            @pl.when(j1 + 1 < nch)
            def _():
                w_copy(j1 + 1).start()

            lhs = grads[j1, pl.ds(pl.multiple_of(l * layer, layer), layer), :]

            @pl.loop(0, feats // tile_f)
            def _(i):
                at = pl.ds(pl.multiple_of(i * tile_f, tile_f), tile_f)
                total[:, at] += lax.dot_general(
                    lhs, wbuf[lax.rem(j1, 2), at, :], (((1,), (1,)), ((), ())),
                    preferred_element_type=jnp.float32)

        @pl.when(s == nch)
        def _():
            term[...] = total[...].astype(term.dtype)

        @pl.when(s == nch + 1)
        def _():
            for o, dev in enumerate(cpeers):
                pltpu.make_async_remote_copy(
                    src_ref=term.at[pl.ds(pl.multiple_of(dev * block, block), block), :],
                    dst_ref=parts.at[o], send_sem=send_t.at[o], recv_sem=recv_t.at[o],
                    device_id={"col": dev}, device_id_type=MESH).start()

        j2 = s - (nd + 1)

        @pl.when(j2 == 0)
        def _():
            for k in range(nd):
                for dev in cpeers:
                    a_wait(k * nc + dev)
            all_copy.start()

        @pl.when(j2 >= 0)
        def _():
            for k in range(1, nd):
                for x in range(nx):
                    g_wait(lax.rem(l + k, nd) * nr + x * CORES + 1 - core, j2)

            @pl.when(j2 >= nch - late)
            def _():
                last_copy(j2 - (nch - late)).start()

        @pl.when((j2 >= 0) & (j2 < nch - late))
        def _():
            @pl.when(j2 >= 2)
            def _():
                o_copy(j2 - 2).wait()

            @pl.loop(0, feats // tile_f)
            def _(i):
                at = pl.ds(pl.multiple_of(i * tile_f, tile_f), tile_f)
                obuf[lax.rem(j2, 2), at, :] = jnp.dot(
                    acts[at, :], grads[j2], preferred_element_type=jnp.float32).astype(obuf.dtype)

            o_copy(j2).start()

        return carry

    lax.fori_loop(0, nch + nd + 1, step, 0)

    result = total[pl.ds(pl.multiple_of(c * block, block), block), :]
    for o, dev in enumerate(cpeers):
        pltpu.make_async_copy(parts.at[o], parts.at[o], recv_t.at[o]).wait()
        result = result + parts[o].astype(jnp.float32)
    ga_ref[...] = result.astype(ga_ref.dtype)

    for o, dev in enumerate(cpeers):
        pltpu.make_async_copy(parts.at[o], parts.at[o], send_t.at[o]).wait()

    def sent_g(way, p):
        pltpu.make_async_copy(whole(p), whole(p), send_g.at[way, p]).wait()

    def sent_a(way, q):
        pltpu.make_async_copy(apiece(q), apiece(q), send_a.at[way, q]).wait()

    for k in range(nd):
        p, q = k * nr + r, k * nc + c

        @pl.when((k <= l) & (l < nd - 1))
        def _(p=p, q=q):
            sent_g(UP, p)
            sent_a(UP, q)

        @pl.when((k >= l) & (l > 0))
        def _(p=p, q=q):
            sent_g(DOWN, p)
            sent_a(DOWN, q)

        for o in range(len(xpeers)):
            sent_g(X + o, p)
        for x in range(nx):
            sent_g(CORE, k * nr + x * CORES + core)
        for o in range(len(cpeers)):
            sent_a(2 + o, q)

    for j in range(max(nch - late - 2, 0), nch - late):
        o_copy(j).wait()
    all_copy.wait()
    for i in range(late):
        last_copy(i).wait()


def finish(tile, ga_ref, done_ref, all_ref, last_ref, ga_out, gw_out,
           gbuf, dbuf, abuf, lbuf, tail, g_sem, in_sem, a_sem, l_sem, out_sem, t_sem):
    feats, early = done_ref.shape
    tiles = feats // tile
    width = gw_out.shape[1]

    def rows(i):
        return pl.ds(pl.multiple_of(i * tile, tile), tile)

    def a_in(i):
        return pltpu.make_async_copy(all_ref.at[rows(i), :], abuf.at[rows(i), :], a_sem.at[i])

    def d_in(i):
        return pltpu.make_async_copy(done_ref.at[rows(i), :], dbuf.at[rows(i), :], in_sem.at[i])

    def d_out(i):
        return pltpu.make_async_copy(
            dbuf.at[rows(i), :], gw_out.at[rows(i), pl.ds(0, early)], out_sem.at[i])

    def t_out(i):
        return pltpu.make_async_copy(
            tail.at[rows(i), :], gw_out.at[rows(i), pl.ds(early, width - early)], t_sem.at[i])

    l_in = pltpu.make_async_copy(last_ref, lbuf, l_sem)
    g_in = pltpu.make_async_copy(ga_ref, gbuf, g_sem.at[0])
    g_out = pltpu.make_async_copy(gbuf, ga_out, g_sem.at[1])
    d_in(0).start()
    l_in.start()
    a_in(0).start()
    g_in.start()
    for i in range(1, tiles):
        a_in(i).start()
        d_in(i).start()
    d_in(0).wait()
    d_out(0).start()
    l_in.wait()
    g_in.wait()
    g_out.start()

    @pl.loop(0, tiles)
    def _(i):
        @pl.when(i > 0)
        def _():
            d_in(i).wait()
            d_out(i).start()

        a_in(i).wait()
        tail[rows(i), :] = jnp.dot(
            abuf[rows(i), :], lbuf[...], preferred_element_type=jnp.float32).astype(tail.dtype)
        t_out(i).start()

    g_out.wait()
    for i in range(tiles):
        d_out(i).wait()
        t_out(i).wait()


def shards(nd, nr, nc, acts, grad_out, weight):
    rows, width = grad_out.shape
    cols = 256
    nch = width // cols
    late = min(4, nch - 2)
    early = (nch - late) * cols
    feats = acts.shape[1]
    layer = nr * rows
    block = layer // nc
    bf16, dma = jnp.bfloat16, pltpu.SemaphoreType.DMA
    anywhere = pl.BlockSpec(memory_space=pl.ANY)
    nx = nr // CORES
    pieces, apieces = nd * nr, nd * nc
    tokens = nd * layer
    limit = 67_043_328
    ga, done, all_acts, last = pl.pallas_call(
        functools.partial(kernel, nd, nr, nc, nch, late, cols),
        out_shape=(
            jax.ShapeDtypeStruct((block, feats), bf16),
            jax.ShapeDtypeStruct((feats, early), bf16),
            jax.ShapeDtypeStruct((feats, tokens), bf16),
            jax.ShapeDtypeStruct((tokens, late * cols), bf16),
        ),
        in_specs=[anywhere] * 3,
        out_specs=(pl.BlockSpec(memory_space=pltpu.VMEM),) + (anywhere,) * 3,
        scratch_shapes=[
            pltpu.VMEM((nch, pieces * rows, cols), bf16),
            pltpu.VMEM((feats, apieces * acts.shape[0]), bf16),
            pltpu.VMEM((layer, feats), jnp.float32),
            pltpu.VMEM((layer, feats), bf16),
            pltpu.VMEM((nc - 1, block, feats), bf16),
            pltpu.VMEM((2, feats, cols), bf16),
            pltpu.VMEM((2, feats, cols), bf16),
            dma((pieces, nch)), dma((apieces,)), dma((nc - 1,)),
            dma((3 + nx - 1, pieces)), dma((2 + nc - 1, apieces)), dma((nc - 1,)),
            dma((2,)), dma((2,)), dma((2,)), dma, dma((late,)),
        ],
        compiler_params=pltpu.CompilerParams(
            collective_id=0, has_side_effects=True, vmem_limit_bytes=limit),
    )(acts.T, grad_out, weight)
    tile = 256
    tiles = feats // tile
    return pl.pallas_call(
        functools.partial(finish, tile),
        out_shape=(
            jax.ShapeDtypeStruct((block, feats), bf16),
            jax.ShapeDtypeStruct((feats, width), bf16),
        ),
        in_specs=[anywhere] * 4,
        out_specs=(anywhere,) * 2,
        scratch_shapes=[
            pltpu.VMEM((block, feats), bf16),
            pltpu.VMEM((feats, early), bf16),
            pltpu.VMEM((feats, tokens), bf16),
            pltpu.VMEM((tokens, width - early), bf16),
            pltpu.VMEM((feats, width - early), bf16),
            dma((2,)), dma((tiles,)), dma((tiles,)), dma, dma((tiles,)), dma((tiles,)),
        ],
        compiler_params=pltpu.CompilerParams(vmem_limit_bytes=limit),
    )(ga, done, all_acts, last)


def solution(mesh):
    nd, nr, nc = mesh.shape["depth"], mesh.shape["row"], mesh.shape["col"]
    in_specs = (P(("depth", "col"), "row"), P(("depth", "row"), "col"), P("row", "col"))
    out_specs = (P(("depth", "col"), "row"), P("row", "col"))
    return jax.shard_map(functools.partial(shards, nd, nr, nc), mesh=mesh,
                         in_specs=in_specs, out_specs=out_specs, check_vma=False)
```

```python
import functools

import jax
import jax.numpy as jnp
from jax import lax
from jax.experimental import pallas as pl
from jax.experimental.pallas import tpu as pltpu
from jax.sharding import PartitionSpec as P

MESH = pl.DeviceIdType.MESH
CORES = 2


def kernel(nd, nr, nc, nch, late, cols, at_ref, g_ref, w_ref, ga_ref, gw_ref, all_ref, last_ref,
           grads, acts, total, term, parts, wbuf, obuf,
           recv_g, recv_a, recv_t, send_g, send_a, send_t, load_sem, w_sem, o_sem, all_sem, last_sem):
    nx = nr // CORES
    l, r, c = lax.axis_index("depth"), lax.axis_index("row"), lax.axis_index("col")
    core = lax.rem(r, CORES)
    xi = lax.div(r, CORES)
    partner = xi * CORES + (1 - core)
    xpeers = [lax.rem(xi + o, nx) * CORES + core for o in range(1, nx)]
    cpeers = [lax.rem(c + o, nc) for o in range(1, nc)]
    rows = g_ref.shape[0]
    width = at_ref.shape[1]
    feats = at_ref.shape[0]
    layer = nr * rows
    block = layer // nc
    UP, DOWN, CORE, X = 0, 1, 2, 3

    def piece(p, j):
        return grads.at[j, pl.ds(pl.multiple_of(p * rows, rows), rows), :]

    def whole(p):
        return grads.at[:, pl.ds(pl.multiple_of(p * rows, rows), rows), :]

    def apiece(q):
        return acts.at[:, pl.ds(pl.multiple_of(q * width, width), width)]

    def g_copy(p, j, way, dev):
        return pltpu.make_async_remote_copy(
            src_ref=piece(p, j), dst_ref=piece(p, j), send_sem=send_g.at[way, p],
            recv_sem=recv_g.at[p, j], device_id=dev, device_id_type=MESH)

    def a_copy(q, way, dev):
        return pltpu.make_async_remote_copy(
            src_ref=apiece(q), dst_ref=apiece(q), send_sem=send_a.at[way, q],
            recv_sem=recv_a.at[q], device_id=dev, device_id_type=MESH)

    def g_wait(p, j):
        pltpu.make_async_copy(piece(p, j), piece(p, j), recv_g.at[p, j]).wait()

    def a_wait(q):
        pltpu.make_async_copy(apiece(q), apiece(q), recv_a.at[q]).wait()

    def to_x(p, j):
        for o, dev in enumerate(xpeers):
            g_copy(p, j, X + o, {"row": dev}).start()

    def to_core(p, j):
        g_copy(p, j, CORE, {"row": partner}).start()

    def to_up(p, j):
        @pl.when(l < nd - 1)
        def _():
            g_copy(p, j, UP, {"depth": l + 1}).start()

    def to_down(p, j):
        @pl.when(l > 0)
        def _():
            g_copy(p, j, DOWN, {"depth": l - 1}).start()

    def w_copy(j):
        return pltpu.make_async_copy(
            w_ref.at[:, pl.ds(pl.multiple_of(j * cols, cols), cols)], wbuf.at[lax.rem(j, 2)],
            w_sem.at[lax.rem(j, 2)])

    def o_copy(j):
        return pltpu.make_async_copy(
            obuf.at[lax.rem(j, 2)], gw_ref.at[:, pl.ds(pl.multiple_of(j * cols, cols), cols)],
            o_sem.at[lax.rem(j, 2)])

    def last_copy(i):
        return pltpu.make_async_copy(
            grads.at[nch - late + i], last_ref.at[:, pl.ds(pl.multiple_of(i * cols, cols), cols)],
            last_sem.at[i])

    all_copy = pltpu.make_async_copy(acts, all_ref, all_sem)

    own = l * nr + r
    mine = l * nc + c

    @pl.loop(0, nch)
    def _(j):
        pltpu.make_async_copy(
            g_ref.at[:, pl.ds(pl.multiple_of(j * cols, cols), cols)], piece(own, j), load_sem.at[0]).start()

    own_acts = pltpu.make_async_copy(at_ref, apiece(mine), load_sem.at[1])
    own_acts.start()
    w_copy(0).start()

    barrier = pltpu.get_barrier_semaphore()
    peers = [{"row": partner}] + [{"row": x} for x in xpeers] + [{"col": y} for y in cpeers]
    for dev in peers:
        pl.semaphore_signal(barrier, inc=1, device_id=dev, device_id_type=MESH)

    @pl.when(l > 0)
    def _():
        pl.semaphore_signal(barrier, inc=1, device_id={"depth": l - 1}, device_id_type=MESH)

    @pl.when(l < nd - 1)
    def _():
        pl.semaphore_signal(barrier, inc=1, device_id={"depth": l + 1}, device_id_type=MESH)

    neighbours = jnp.where(l > 0, 1, 0) + jnp.where(l < nd - 1, 1, 0)
    pl.semaphore_wait(barrier, len(peers) + neighbours)

    own_acts.wait()
    pltpu.make_async_copy(whole(own), whole(own), load_sem.at[0]).wait()

    @pl.when(l < nd - 1)
    def _():
        a_copy(mine, UP, {"depth": l + 1}).start()

    @pl.when(l > 0)
    def _():
        a_copy(mine, DOWN, {"depth": l - 1}).start()

    for o, dev in enumerate(cpeers):
        a_copy(mine, 2 + o, {"col": dev}).start()

    for j in range(min(1, nch)):
        to_up(own, j)
        to_down(own, j)

    @pl.loop(0, nch)
    def _(j):
        to_x(own, j)
        to_core(own, j)

    total[...] = jnp.zeros_like(total)

    tile_f = 256

    def step(s, carry):
        @pl.when(s + 1 < nch)
        def _():
            to_up(own, s + 1)
            to_down(own, s + 1)

        for d in range(1, nd):
            j = s - d
            live = (j >= 0) & (j < nch)
            for sign, onward in ((-1, to_up), (1, to_down)):
                src = l + sign * d
                there = (src >= 0) if sign < 0 else (src < nd)

                @pl.when(live & there)
                def _(j=j, src=src, onward=onward):
                    p = src * nr + r
                    g_wait(p, j)
                    onward(p, j)
                    to_x(p, j)
                    to_core(p, j)

                @pl.when((s == d) & there)
                def _(src=src, sign=sign):
                    q = src * nc + c
                    a_wait(q)
                    if sign < 0:
                        @pl.when(l < nd - 1)
                        def _():
                            a_copy(q, UP, {"depth": l + 1}).start()
                    else:
                        @pl.when(l > 0)
                        def _():
                            a_copy(q, DOWN, {"depth": l - 1}).start()
                    for o, dev in enumerate(cpeers):
                        a_copy(q, 2 + o, {"col": dev}).start()

        for d in range(0, nd):
            j = s - (d + 1 if d else 0)
            live = (j >= 0) & (j < nch)
            for sign in ((-1, 1) if d else (1,)):
                src = l + sign * d
                there = (src >= 0) & (src < nd)

                @pl.when(live & there)
                def _(j=j, src=src):
                    for x in xpeers:
                        g_wait(src * nr + x, j)
                        to_core(src * nr + x, j)

        j1 = s - 1

        @pl.when((j1 >= 0) & (j1 < nch))
        def _():
            for x in range(nx):
                g_wait(l * nr + x * CORES + 1 - core, j1)
            w_copy(j1).wait()

            @pl.when(j1 + 1 < nch)
            def _():
                w_copy(j1 + 1).start()

            lhs = grads[j1, pl.ds(pl.multiple_of(l * layer, layer), layer), :]

            @pl.loop(0, feats // tile_f)
            def _(i):
                at = pl.ds(pl.multiple_of(i * tile_f, tile_f), tile_f)
                total[:, at] += lax.dot_general(
                    lhs, wbuf[lax.rem(j1, 2), at, :], (((1,), (1,)), ((), ())),
                    preferred_element_type=jnp.float32)

        @pl.when(s == nch)
        def _():
            term[...] = total[...].astype(term.dtype)

        @pl.when(s == nch + 1)
        def _():
            for o, dev in enumerate(cpeers):
                pltpu.make_async_remote_copy(
                    src_ref=term.at[pl.ds(pl.multiple_of(dev * block, block), block), :],
                    dst_ref=parts.at[o], send_sem=send_t.at[o], recv_sem=recv_t.at[o],
                    device_id={"col": dev}, device_id_type=MESH).start()

        j2 = s - (nd + 1)

        @pl.when(j2 == 0)
        def _():
            for k in range(nd):
                for dev in cpeers:
                    a_wait(k * nc + dev)
            all_copy.start()

        @pl.when(j2 >= 0)
        def _():
            for k in range(1, nd):
                for x in range(nx):
                    g_wait(lax.rem(l + k, nd) * nr + x * CORES + 1 - core, j2)

            @pl.when(j2 >= nch - late)
            def _():
                last_copy(j2 - (nch - late)).start()

        @pl.when((j2 >= 0) & (j2 < nch - late))
        def _():
            @pl.when(j2 >= 2)
            def _():
                o_copy(j2 - 2).wait()

            @pl.loop(0, feats // tile_f)
            def _(i):
                at = pl.ds(pl.multiple_of(i * tile_f, tile_f), tile_f)
                obuf[lax.rem(j2, 2), at, :] = jnp.dot(
                    acts[at, :], grads[j2], preferred_element_type=jnp.float32).astype(obuf.dtype)

            o_copy(j2).start()

        return carry

    lax.fori_loop(0, nch + nd + 1, step, 0)

    result = total[pl.ds(pl.multiple_of(c * block, block), block), :]
    for o, dev in enumerate(cpeers):
        pltpu.make_async_copy(parts.at[o], parts.at[o], recv_t.at[o]).wait()
        result = result + parts[o].astype(jnp.float32)
    ga_ref[...] = result.astype(ga_ref.dtype)

    for o, dev in enumerate(cpeers):
        pltpu.make_async_copy(parts.at[o], parts.at[o], send_t.at[o]).wait()

    def sent_g(way, p):
        pltpu.make_async_copy(whole(p), whole(p), send_g.at[way, p]).wait()

    def sent_a(way, q):
        pltpu.make_async_copy(apiece(q), apiece(q), send_a.at[way, q]).wait()

    for k in range(nd):
        p, q = k * nr + r, k * nc + c

        @pl.when((k <= l) & (l < nd - 1))
        def _(p=p, q=q):
            sent_g(UP, p)
            sent_a(UP, q)

        @pl.when((k >= l) & (l > 0))
        def _(p=p, q=q):
            sent_g(DOWN, p)
            sent_a(DOWN, q)

        for o in range(len(xpeers)):
            sent_g(X + o, p)
        for x in range(nx):
            sent_g(CORE, k * nr + x * CORES + core)
        for o in range(len(cpeers)):
            sent_a(2 + o, q)

    for j in range(max(nch - late - 2, 0), nch - late):
        o_copy(j).wait()
    all_copy.wait()
    for i in range(late):
        last_copy(i).wait()


def finish(tile, ga_ref, done_ref, all_ref, last_ref, ga_out, gw_out,
           gbuf, dbuf, abuf, lbuf, tail, g_sem, in_sem, a_sem, l_sem, out_sem, t_sem):
    feats, early = done_ref.shape
    tiles = feats // tile
    width = gw_out.shape[1]

    def rows(i):
        return pl.ds(pl.multiple_of(i * tile, tile), tile)

    def a_in(i):
        return pltpu.make_async_copy(all_ref.at[rows(i), :], abuf.at[rows(i), :], a_sem.at[i])

    def d_in(i):
        return pltpu.make_async_copy(done_ref.at[rows(i), :], dbuf.at[rows(i), :], in_sem.at[i])

    def d_out(i):
        return pltpu.make_async_copy(
            dbuf.at[rows(i), :], gw_out.at[rows(i), pl.ds(0, early)], out_sem.at[i])

    def t_out(i):
        return pltpu.make_async_copy(
            tail.at[rows(i), :], gw_out.at[rows(i), pl.ds(early, width - early)], t_sem.at[i])

    l_in = pltpu.make_async_copy(last_ref, lbuf, l_sem)
    g_in = pltpu.make_async_copy(ga_ref, gbuf, g_sem.at[0])
    g_out = pltpu.make_async_copy(gbuf, ga_out, g_sem.at[1])
    d_in(0).start()
    l_in.start()
    a_in(0).start()
    g_in.start()
    for i in range(1, tiles):
        a_in(i).start()
        d_in(i).start()
    d_in(0).wait()
    d_out(0).start()
    l_in.wait()
    g_in.wait()
    g_out.start()

    @pl.loop(0, tiles)
    def _(i):
        @pl.when(i > 0)
        def _():
            d_in(i).wait()
            d_out(i).start()

        a_in(i).wait()
        tail[rows(i), :] = jnp.dot(
            abuf[rows(i), :], lbuf[...], preferred_element_type=jnp.float32).astype(tail.dtype)
        t_out(i).start()

    g_out.wait()
    for i in range(tiles):
        d_out(i).wait()
        t_out(i).wait()


def shards(nd, nr, nc, acts, grad_out, weight):
    rows, width = grad_out.shape
    cols = 512 if width % 512 == 0 else 256
    nch = width // cols
    late = max(min(2, nch - 2), 1)
    early = (nch - late) * cols
    feats = acts.shape[1]
    layer = nr * rows
    block = layer // nc
    bf16, dma = jnp.bfloat16, pltpu.SemaphoreType.DMA
    anywhere = pl.BlockSpec(memory_space=pl.ANY)
    nx = nr // CORES
    pieces, apieces = nd * nr, nd * nc
    tokens = nd * layer
    limit = 67_043_328
    ga, done, all_acts, last = pl.pallas_call(
        functools.partial(kernel, nd, nr, nc, nch, late, cols),
        out_shape=(
            jax.ShapeDtypeStruct((block, feats), bf16),
            jax.ShapeDtypeStruct((feats, early), bf16),
            jax.ShapeDtypeStruct((feats, tokens), bf16),
            jax.ShapeDtypeStruct((tokens, late * cols), bf16),
        ),
        in_specs=[anywhere] * 3,
        out_specs=(pl.BlockSpec(memory_space=pltpu.VMEM),) + (anywhere,) * 3,
        scratch_shapes=[
            pltpu.VMEM((nch, pieces * rows, cols), bf16),
            pltpu.VMEM((feats, apieces * acts.shape[0]), bf16),
            pltpu.VMEM((layer, feats), jnp.float32),
            pltpu.VMEM((layer, feats), bf16),
            pltpu.VMEM((nc - 1, block, feats), bf16),
            pltpu.VMEM((2, feats, cols), bf16),
            pltpu.VMEM((2, feats, cols), bf16),
            dma((pieces, nch)), dma((apieces,)), dma((nc - 1,)),
            dma((3 + nx - 1, pieces)), dma((2 + nc - 1, apieces)), dma((nc - 1,)),
            dma((2,)), dma((2,)), dma((2,)), dma, dma((late,)),
        ],
        compiler_params=pltpu.CompilerParams(
            collective_id=0, has_side_effects=True, vmem_limit_bytes=limit),
    )(acts.T, grad_out, weight)
    tile = 256
    tiles = feats // tile
    return pl.pallas_call(
        functools.partial(finish, tile),
        out_shape=(
            jax.ShapeDtypeStruct((block, feats), bf16),
            jax.ShapeDtypeStruct((feats, width), bf16),
        ),
        in_specs=[anywhere] * 4,
        out_specs=(anywhere,) * 2,
        scratch_shapes=[
            pltpu.VMEM((block, feats), bf16),
            pltpu.VMEM((feats, early), bf16),
            pltpu.VMEM((feats, tokens), bf16),
            pltpu.VMEM((tokens, width - early), bf16),
            pltpu.VMEM((feats, width - early), bf16),
            dma((2,)), dma((tiles,)), dma((tiles,)), dma, dma((tiles,)), dma((tiles,)),
        ],
        compiler_params=pltpu.CompilerParams(vmem_limit_bytes=limit),
    )(ga, done, all_acts, last)


def solution(mesh):
    nd, nr, nc = mesh.shape["depth"], mesh.shape["row"], mesh.shape["col"]
    in_specs = (P(("depth", "col"), "row"), P(("depth", "row"), "col"), P("row", "col"))
    out_specs = (P(("depth", "col"), "row"), P("row", "col"))
    return jax.shard_map(functools.partial(shards, nd, nr, nc), mesh=mesh,
                         in_specs=in_specs, out_specs=out_specs, check_vma=False)
```
